512 devices in a mesh: wide: 32 (over x, z_hi, core), narrow: 16 (over y, z_lo).
Axes of the slice: x: 4, y: 4, z: 16 (z_hi: 4, z_lo: 4; z = z_hi * 4 + z_lo), core: 2. Of those that a mesh axis runs over, the one named last changes fastest.
Arguments:
- features: bfloat16 [262144, 512], P(('wide', 'narrow')), may hold values from -6 to 6
- stripe_owner: int32 [16, 2], replicated, may hold values from 0 to 31
- dense_weight: int32 [262144, 1024], P(('wide', 'narrow')), may hold values from 0 to 3
- sparse_weight: int32 [512, 16, 128, 128], P(('wide', 'narrow')), may hold values from 0 to 3
- send_blocks: int32 [512, 16, 2], P(('wide', 'narrow')), may hold values from -1 to 3, as said below
- target_block: int32 [512, 16, 2], P(('wide', 'narrow')), may hold values from 0 to 3
- first_weight: bfloat16 [512, 2048], P('wide'), may hold values from -0.25 to 0.25
- second_weight: bfloat16 [2048, 512], P('wide'), may hold values from -0.125 to 0.125
Outputs:
- updated: bfloat16 [262144, 512], P(('wide', 'narrow'))
The draws below stay inside these ranges and needn't reach their ends.
Inputs may be any that keep to these rules, and one draw needn't show every extreme that they name: `send_blocks`: entry [d, p, s] names a local row block of device d for slot s to partition p of d's wide group, -1 marks an empty slot, filled slots come first; in every wide group one partition receives 2 blocks from every member.
All inputs are finite; a program needn't handle non-finite values.
Results may differ from the reference program's by a relative error of at most 0.0057.
Values may be sent and summed in bfloat16 or wider, within the bound.
A program may use at most 128 MiB of HBM per device.

```python
import jax
import jax.numpy as jnp
from jax import lax

D = 512
FF = 2048
ROWS = 512
BLOCK = 128
STRIPES = 2
CAP = 2
BLOCKS = 4
DEVICES_ALL = 512
NODES = 262144
N_WIDE = 32
N_NARROW = 16


def draw_send_blocks(key, part):
    key_count = jax.random.fold_in(key, 11)
    key_hot = jax.random.fold_in(key, 12)
    key_pick = jax.random.fold_in(key, 13)
    counts = jax.random.randint(key_count, (DEVICES_ALL, N_NARROW), 0, CAP + 1)
    groups = DEVICES_ALL // N_NARROW
    hottest = jax.random.randint(key_hot, (groups,), 0, N_NARROW)
    group_of = jnp.arange(DEVICES_ALL) // N_NARROW
    column = jnp.arange(N_NARROW)
    is_hot = column[None, :] == hottest[group_of][:, None]
    counts = jnp.where(is_hot, CAP, counts)
    chosen = jax.random.randint(key_pick, (DEVICES_ALL, N_NARROW, CAP), 0, ROWS // BLOCK)
    filled = jnp.arange(CAP)[None, None, :] < counts[:, :, None]
    return jnp.where(filled, chosen, -1).astype(jnp.int32)


def place_ends(drawn, rng, low, top_value):
    dims = drawn.shape
    spot = [jax.random.randint(jax.random.fold_in(rng, axis), (), 0, dims[axis]) for axis in range(len(dims))]
    drawn = drawn.at[tuple(spot)].set(low)
    longest = dims.index(max(dims))
    spot[longest] = (spot[longest] + 1) % dims[longest]
    return drawn.at[tuple(spot)].set(top_value)


def levels(own_key, shape, shards, least, largest):
    def one(axis_at, blocks):
        draws = jax.random.uniform(jax.random.fold_in(jax.random.fold_in(own_key, 6), axis_at), (blocks,), jnp.float32, least / len(shards), largest / len(shards))
        return jnp.repeat(jnp.exp(draws), shape[axis_at] // blocks).reshape((-1,) + (1,) * (len(shape) - axis_at - 1))

    factor_of = one(*shards[0])
    for cut in shards[1:]:
        factor_of = factor_of * one(*cut)
    return factor_of


def normal_values(key, shape, deviation, most, cuts=(), held_as=jnp.bfloat16):
    values = jax.random.normal(key, shape, jnp.float32) * deviation
    if len(cuts) > 0:
        values = levels(key, shape, cuts, -0.22, 0.18) * values
    return jnp.clip(values, min=-most, max=most).astype(held_as)


def setup_inputs(seed: int = 0) -> dict:
    key_of = jax.random.split(jax.random.key(seed), 9)
    return {
        "features": normal_values(key_of[0], (NODES, D), 1.0, 6.0, ((0, 512),)),
        "stripe_owner": place_ends(jax.random.randint(key_of[1], (N_NARROW, STRIPES), 0, N_WIDE), jax.random.fold_in(key_of[1], 1), 0, N_WIDE - 1).astype(jnp.int32),
        "dense_weight": place_ends(jax.random.randint(key_of[2], (NODES, STRIPES * ROWS), 0, 4), jax.random.fold_in(key_of[2], 1), 0, 3).astype(jnp.int32),
        "sparse_weight": place_ends(jax.random.randint(key_of[3], (DEVICES_ALL, N_NARROW, BLOCK, BLOCK), 0, 4), jax.random.fold_in(key_of[3], 1), 0, 3).astype(jnp.int32),
        "send_blocks": draw_send_blocks(jax.random.fold_in(key_of[8], 71), 0),
        "target_block": place_ends(jax.random.randint(key_of[5], (DEVICES_ALL, N_NARROW, CAP), 0, BLOCKS), jax.random.fold_in(key_of[5], 1), 0, BLOCKS - 1).astype(jnp.int32),
        "first_weight": normal_values(key_of[6], (D, FF), D ** -0.5, 0.25, ((0, 32),)),
        "second_weight": normal_values(key_of[7], (FF, D), FF ** -0.5, 0.125, ((0, 32),)),
    }


def reference(features, stripe_owner, dense_weight, sparse_weight, send_blocks, target_block, first_weight, second_weight):
    feature_rows = features.reshape(DEVICES_ALL, ROWS, D)
    block_grid = features.reshape(DEVICES_ALL, BLOCKS, BLOCK, D)
    dense_rows = dense_weight.reshape(DEVICES_ALL, ROWS, STRIPES * ROWS)
    highest = lax.Precision.HIGHEST

    def device_update(device):
        wide_index = device // N_NARROW
        narrow_index = device % N_NARROW
        owners = stripe_owner[narrow_index]
        stripes = feature_rows[owners * N_NARROW + narrow_index].reshape(STRIPES * ROWS, D)
        dense_local = dense_rows[device]
        dense_sum = jnp.dot(dense_local.astype(jnp.bfloat16), stripes, preferred_element_type=jnp.float32)
        source = (wide_index * N_NARROW + jnp.arange(N_NARROW)).astype(jnp.int32)
        listed = send_blocks[source, narrow_index, :]
        present = listed >= 0
        chosen = block_grid[source[:, None], jnp.maximum(listed, 0)]
        tile_weights = sparse_weight[device].astype(jnp.float32)
        products = jnp.einsum('pij,pcjd->pcid', tile_weights, chosen.astype(jnp.float32), precision=highest)
        products = jnp.where(present[:, :, None, None], products, jnp.zeros((), products.dtype))
        routed = (target_block[device][:, :, None] == jnp.arange(BLOCKS)[None, None, :]) & present[:, :, None]
        routed = routed.astype(jnp.float32)
        sparse_sum = jnp.einsum('pcb,pcid->bid', routed, products, precision=highest).reshape(ROWS, D)
        row_weight = lax.optimization_barrier(jnp.sum(tile_weights, axis=2))
        sparse_degree = jnp.einsum('pcb,pi->bi', routed, row_weight, precision=highest).reshape(ROWS)
        degree = 1.0 + lax.optimization_barrier(jnp.sum(dense_local, axis=1)).astype(jnp.float32) + sparse_degree
        combined = (feature_rows[device].astype(jnp.float32) + (dense_sum + sparse_sum) / jnp.sqrt(degree)[:, None]).astype(jnp.bfloat16)
        hidden = jax.nn.relu(jnp.dot(combined, first_weight, preferred_element_type=jnp.float32)).astype(jnp.bfloat16)
        return jnp.dot(hidden, second_weight, preferred_element_type=jnp.float32).astype(jnp.bfloat16)
    updated = lax.map(device_update, jnp.arange(DEVICES_ALL, dtype=jnp.int32))
    return updated.reshape(NODES, D)
```

```python
import jax
import jax.numpy as jnp
from jax import lax
from jax.experimental import pallas as pl
from jax.experimental.pallas import tpu as pltpu
from jax.sharding import PartitionSpec as P

MESH = pl.DeviceIdType.MESH
BF = jnp.bfloat16
F32 = jnp.float32
N_SEND = 128
N_RECV = 128


def kernel(
    owner_ref, target_ref, f_ref, flag_ref, w1_in, w2_in, dense_hbm, tile_hbm, out_ref,
    zf, fl, gate, tx, fwd, got_x, route, w1, w2, partner_f, cand, rxh, rxp, candz, rzh, rzp,
    stripes, dense, tiles, dense16, acc, deg, comb, send_sem, recv_sem, load_sem,
):
    w, n = lax.axis_index("wide"), lax.axis_index("narrow")
    x, h, c = lax.div(w, 8), lax.rem(lax.div(w, 2), 4), lax.rem(w, 2)
    y, i = lax.div(n, 4), lax.rem(n, 4)

    def up(v, by=1):
        return lax.rem(v + by, 4)

    def at(xx=x, hh=h, cc=c, yy=y, ii=i):
        return {"wide": xx * 8 + hh * 2 + cc, "narrow": yy * 4 + ii}

    x_r, x_l, x_o = up(x), up(x, 3), up(x, 2)
    h_r, h_l, h_o = up(h), up(h, 3), up(h, 2)
    y_r, y_l, y_o = up(y), up(y, 3), up(y, 2)
    right_x, left_x = at(xx=x_r), at(xx=x_l)
    right_h, left_h = at(hh=h_r), at(hh=h_l)
    right_y, left_y, far_y = at(yy=y_r), at(yy=y_l), at(yy=y_o)
    partner = at(cc=1 - c)
    z = h * 4 + i
    z_r, z_l = lax.rem(z + 1, 16), lax.rem(z + 15, 16)
    right_z = at(hh=lax.div(z_r, 4), ii=lax.rem(z_r, 4))
    left_z = at(hh=lax.div(z_l, 4), ii=lax.rem(z_l, 4))
    line = [at(ii=up(i, k)) for k in (1, 2, 3)]

    pending = []
    count = {"send": 0, "recv": 0}

    def slots(kind, k=1):
        count[kind] += k
        return count[kind] - k

    def send(src, dst, recv, device, cond=None):
        slot = slots("send")

        def copy():
            return pltpu.make_async_remote_copy(
                src_ref=src, dst_ref=dst, send_sem=send_sem.at[slot], recv_sem=recv_sem.at[recv],
                device_id=device, device_id_type=MESH,
            )

        if cond is None:
            copy().start()
        else:
            pl.when(cond)(lambda: copy().start())
        pending.append((copy, cond))

    def arrived(dst, recv):
        pltpu.make_async_remote_copy(
            src_ref=dst, dst_ref=dst, send_sem=send_sem.at[0], recv_sem=recv_sem.at[recv],
            device_id=partner, device_id_type=MESH,
        ).wait_recv()

    loads = [
        pltpu.make_async_copy(dense_hbm, dense, load_sem.at[0]),
        pltpu.make_async_copy(tile_hbm, tiles, load_sem.at[1]),
    ]
    for load in loads:
        load.start()
    barrier = pltpu.get_barrier_semaphore()
    peers = [right_x, left_x, right_h, left_h, right_y, left_y, far_y, partner, right_z, left_z, *line]
    for peer in peers:
        pl.semaphore_signal(barrier, inc=1, device_id=peer, device_id_type=MESH)
    fl[n] = flag_ref[...]
    acc[...] = jnp.zeros_like(acc)
    pl.semaphore_wait(barrier, len(peers))

    r_flag = slots("recv", 4)
    r_flag_y = slots("recv", 4)
    r_f = slots("recv", 4)
    r_part = slots("recv")
    r_swap = slots("recv")
    r_y = slots("recv", 24)
    r_chain = slots("recv", 6)
    r_wx = slots("recv", 24)
    r_wc = slots("recv", 8)
    r_s = slots("recv", 16)

    def load_own_weights():
        pass

    def w_own():
        for part, (src, buf) in enumerate(((w1_in, w1), (w2_in, w2))):
            send(src, buf.at[x, h, c], r_chain + part, right_z, i == 3)
            send(src, buf.at[x, h, c], r_chain + 2 + part, left_z, i == 0)

    def w_x_own():
        for part, (src, buf) in enumerate(((w1_in, w1), (w2_in, w2))):
            send(src, buf.at[x, h, c], r_wx + part, right_x)
            send(src, buf.at[x, h, c], r_wx + 2 + part, left_x)

    def chain_near(position):
        @pl.when(i == position)
        def _():
            arrived(w1.at[x, h_l, c], r_chain + 0)
            arrived(w2.at[x, h_l, c], r_chain + 1)

        near_l = i == position
        near_r = i == 3 - position
        if position < 3:
            send(w1.at[x, h_l, c], w1.at[x, h_l, c], r_chain + 0, right_z, near_l)
            send(w2.at[x, h_l, c], w2.at[x, h_l, c], r_chain + 1, right_z, near_l)
        else:
            send(w1.at[x, h_l, c], w1.at[x, h_l, c], r_chain + 4, right_z, near_l)

        @pl.when(near_r)
        def _():
            arrived(w1.at[x, h_r, c], r_chain + 2)
            arrived(w2.at[x, h_r, c], r_chain + 3)

        if position < 3:
            send(w1.at[x, h_r, c], w1.at[x, h_r, c], r_chain + 2, left_z, near_r)
            send(w2.at[x, h_r, c], w2.at[x, h_r, c], r_chain + 3, left_z, near_r)
        else:
            send(w2.at[x, h_r, c], w2.at[x, h_r, c], r_chain + 5, left_z, near_r)

    def chain_far(position):
        near_l = i == position
        near_r = i == 3 - position

        @pl.when(near_l)
        def _():
            arrived(w1.at[x, h_o, c], r_chain + 4)

        if position < 3:
            send(w1.at[x, h_o, c], w1.at[x, h_o, c], r_chain + 4, right_z, near_l)

        @pl.when(near_r)
        def _():
            arrived(w2.at[x, h_o, c], r_chain + 5)

        if position < 3:
            send(w2.at[x, h_o, c], w2.at[x, h_o, c], r_chain + 5, left_z, near_r)

    def w_x(group, hh):
        base = r_wx + 6 * group
        for part, buf in enumerate((w1, w2)):
            send(buf.at[x, hh, c], buf.at[x, hh, c], base + part, right_x)
            send(buf.at[x, hh, c], buf.at[x, hh, c], base + 2 + part, left_x)

    def w_x_relay(group, hh):
        base = r_wx + 6 * group
        arrived(w1.at[x_l, hh, c], base + 0)
        send(w1.at[x_l, hh, c], w1.at[x_l, hh, c], base + 4, right_x)
        arrived(w2.at[x_r, hh, c], base + 3)
        send(w2.at[x_r, hh, c], w2.at[x_r, hh, c], base + 5, left_x)

    def w_x_done(group, hh):
        base = r_wx + 6 * group
        arrived(w2.at[x_l, hh, c], base + 1)
        arrived(w1.at[x_r, hh, c], base + 2)
        arrived(w1.at[x_o, hh, c], base + 4)
        arrived(w2.at[x_o, hh, c], base + 5)
        send(w1.at[:, hh, c], w1.at[:, hh, c], r_wc + 2 * group, partner)
        send(w2.at[:, hh, c], w2.at[:, hh, c], r_wc + 2 * group + 1, partner)

    def w_core(group, hh):
        arrived(w1.at[:, hh, 1 - c], r_wc + 2 * group)
        arrived(w2.at[:, hh, 1 - c], r_wc + 2 * group + 1)

    def s_start():
        send(f_ref, partner_f, r_part, partner)

    def s_mask():
        owner = owner_ref[c, n]
        mine = jnp.where(owner == w, 1.0, 0.0)
        other = jnp.where(owner == w + 1 - 2 * c, 1.0, 0.0)
        arrived(partner_f, r_part)
        for q in range(4):
            rows = pl.ds(q * 128, 128)
            cand[q] = (f_ref[rows, :].astype(F32) * mine + partner_f[rows, :].astype(F32) * other).astype(BF)

    def rs_first(buf, half, me_o, rbuf, base, right, left):
        send(buf.at[me_o, pl.ds(0, half)], rbuf.at[0], base + 0, right)
        send(buf.at[me_o, pl.ds(half, half)], rbuf.at[1], base + 1, left)

    def rs_second(buf, half, me_r, me_l, rbuf, pbuf, base, right, left):
        arrived(rbuf.at[0], base + 0)
        buf[me_r, 0:half] = buf[me_r, 0:half] + rbuf[0]
        arrived(rbuf.at[1], base + 1)
        buf[me_l, half:] = buf[me_l, half:] + rbuf[1]
        send(buf.at[me_r], pbuf.at[0], base + 2, right)
        send(buf.at[me_l], pbuf.at[1], base + 3, left)

    def s_x1():
        rs_first(cand, 64, x_o, rxh, r_s + 0, right_x, left_x)

    def s_x2():
        rs_second(cand, 64, x_r, x_l, rxh, rxp, r_s + 0, right_x, left_x)

    def s_z1():
        arrived(rxp.at[0], r_s + 2)
        arrived(rxp.at[1], r_s + 3)
        candz[...] = (cand[x] + rxp[0] + rxp[1]).reshape(4, 32, 512)
        rs_first(candz, 16, h_o, rzh, r_s + 4, right_h, left_h)

    def s_z2():
        rs_second(candz, 16, h_r, h_l, rzh, rzp, r_s + 4, right_h, left_h)

    def s_z3():
        arrived(rzp.at[0], r_s + 6)
        arrived(rzp.at[1], r_s + 7)
        stripes[c, x, h] = candz[h] + rzp[0] + rzp[1]
        piece = stripes.at[c, x, h]
        send(piece, piece, r_s + 8, right_h)
        send(piece, piece, r_s + 9, left_h)

    def s_z4():
        arrived(stripes.at[c, x, h_l], r_s + 8)
        half = stripes.at[c, x, h_l, pl.ds(0, 16)]
        send(half, half, r_s + 10, right_h)
        arrived(stripes.at[c, x, h_r], r_s + 9)
        half = stripes.at[c, x, h_r, pl.ds(16, 16)]
        send(half, half, r_s + 11, left_h)

    def s_x3():
        arrived(stripes.at[c, x, h_o, pl.ds(0, 16)], r_s + 10)
        arrived(stripes.at[c, x, h_o, pl.ds(16, 16)], r_s + 11)
        piece = stripes.at[c, x]
        send(piece, piece, r_s + 12, right_x)
        send(piece, piece, r_s + 13, left_x)

    def s_x4():
        arrived(stripes.at[c, x_l], r_s + 12)
        half = stripes.at[c, x_l, pl.ds(0, 2)]
        send(half, half, r_s + 14, right_x)
        arrived(stripes.at[c, x_r], r_s + 13)
        half = stripes.at[c, x_r, pl.ds(2, 2)]
        send(half, half, r_s + 15, left_x)

    def s_swap():
        arrived(stripes.at[c, x_o, pl.ds(0, 2)], r_s + 14)
        arrived(stripes.at[c, x_o, pl.ds(2, 2)], r_s + 15)
        send(stripes.at[c], stripes.at[c], r_swap, partner)

    def s_done():
        arrived(stripes.at[1 - c], r_swap)

    def flags_z():
        for k in (1, 2, 3):
            send(flag_ref, fl.at[n], r_flag + i, line[k - 1])

    def flags_y():
        for k in (1, 2, 3):
            j = up(i, k)
            arrived(fl.at[y * 4 + j], r_flag + j)
        row = fl.at[pl.ds(y * 4, 4)]
        for device in (right_y, left_y, far_y):
            send(row, row, r_flag_y + y, device)

    def flags_done():
        for k in (1, 2, 3):
            yy = up(y, k)
            arrived(fl.at[pl.ds(yy * 4, 4)], r_flag_y + yy)

    first = jnp.where(i == 0, 1, i - 1)
    second = jnp.where(i == 0, 2, jnp.where(i == 1, 2, jnp.where(i == 2, 3, 1)))
    third = jnp.where(i < 2, 3, 0)
    order = [i, first, second, third]

    def f_own():
        send(f_ref, zf.at[i], r_f + i, right_z, i < 3)
        send(f_ref, zf.at[i], r_f + i, left_z, i > 0)

    def f_relay(k):
        j = order[k]
        arrived(zf.at[j], r_f + j)
        send(zf.at[j], zf.at[j], r_f + j, right_z, (j < i) & (i < 3))
        send(zf.at[j], zf.at[j], r_f + j, left_z, (j > i) & (i > 0))

    def pick(k):
        j = order[k]
        source = f_ref if k == 0 else zf.at[j]
        tile = fl[y * 4 + j]
        lane = lax.broadcasted_iota(jnp.int32, (8, 128), 1)
        for d in range(4):
            column = up(y, d) * 4 + i
            value = jnp.sum(jnp.where(lane == column, tile, 0.0), axis=1, keepdims=True)
            for s in range(2):
                one = jnp.broadcast_to(value[s : s + 1, :], (16, 128))
                for e in range(4):
                    gate[(d * 2 + s) * 4 + e] = jnp.where(one == e + 1.0, 1.0, 0.0).astype(BF)

        @pl.loop(0, 8)
        def _(r):
            blocks = [source[pl.ds(pl.multiple_of(e * 128 + r * 16, 16), 16), :] for e in range(4)]
            for d in range(4):
                for s in range(2):
                    total = None
                    for e in range(4):
                        g = gate[(d * 2 + s) * 4 + e]
                        term = blocks[e] * jnp.concatenate([g, g, g, g], axis=1)
                        total = term if total is None else total + term
                    rows = pl.ds(pl.multiple_of(r * 16, 16), 16)
                    if d == 0:
                        got_x[y * 4 + j, s, rows, :] = total
                    else:
                        tx[k, d - 1, s, rows, :] = total

    def y_send(k):
        p = y * 4 + order[k]
        base = r_y + 6 * k
        send(tx.at[k, 1, 0], fwd.at[k, 0], base + 2, right_y)
        send(tx.at[k, 1, 1], fwd.at[k, 1], base + 3, left_y)
        send(tx.at[k, 0], got_x.at[p], base + 0, right_y)
        send(tx.at[k, 2], got_x.at[p], base + 1, left_y)

    def y_relay(k):
        base = r_y + 6 * k
        arrived(fwd.at[k, 0], base + 2)
        send(fwd.at[k, 0], got_x.at[y_l * 4 + order[k], 0], base + 4, right_y)
        arrived(fwd.at[k, 1], base + 3)
        send(fwd.at[k, 1], got_x.at[y_r * 4 + order[k], 1], base + 5, left_y)

    def y_done(k):
        base = r_y + 6 * k
        arrived(got_x.at[y_l * 4 + order[k]], base + 0)
        arrived(got_x.at[y_r * 4 + order[k]], base + 1)
        arrived(got_x.at[y_o * 4 + order[k], 0], base + 4)
        arrived(got_x.at[y_o * 4 + order[k], 1], base + 5)

    def prepare():
        for load in loads:
            load.wait()
        for q in range(4):
            rows = pl.ds(q * 128, 128)
            block = dense[rows, :]
            dense16[rows, :] = block.astype(F32).astype(BF)
            total = 1.0 + jnp.sum(block.astype(F32), axis=1, keepdims=True)
            deg[rows, :] = jnp.broadcast_to(total, (128, 128))

        @pl.loop(0, 16)
        def _(p):
            tile = tiles[p].astype(F32)
            for s in range(2):
                for b in range(4):
                    hit = jnp.where(target_ref[s, p] == b, 1.0, 0.0)
                    route[p, pl.ds(b * 128, 128), pl.ds(s * 128, 128)] = (tile * hit).astype(BF)

    def degrees():
        lane = lax.broadcasted_iota(jnp.int32, (8, 128), 1)

        @pl.loop(0, 16)
        def _(p):
            rows = jnp.sum(tiles[p].astype(F32), axis=1, keepdims=True)
            value = jnp.sum(jnp.where(lane == n, fl[p], 0.0), axis=1, keepdims=True)
            present = jnp.minimum(value, 1.0)
            for b in range(4):
                weight = jnp.zeros((1, 1), F32)
                for s in range(2):
                    hit = jnp.where(target_ref[s, p] == b, 1.0, 0.0)
                    weight = weight + present[s : s + 1, :] * hit
                where = pl.ds(b * 128, 128)
                deg[where, :] = deg[where, :] + jnp.broadcast_to(rows * weight, (128, 128))

    def sparse(k):
        @pl.loop(0, 4)
        def _(yy):
            p = yy * 4 + order[k]
            block = got_x[p].reshape(256, 512)
            acc[...] += jnp.dot(route[p], block, preferred_element_type=F32)

    def dense_part():
        for k in range(2):
            block = stripes[k].reshape(512, 512)
            acc[...] += jnp.dot(dense16[:, k * 512 : (k + 1) * 512], block, preferred_element_type=F32)

    def combine():
        for q in range(4):
            rows = pl.ds(q * 128, 128)
            scale = 1.0 / jnp.sqrt(deg[rows, :])
            scale = jnp.concatenate([scale, scale, scale, scale], axis=1)
            comb[rows, :] = (f_ref[rows, :].astype(F32) + acc[rows, :] * scale).astype(BF)

    def mlp():
        acc[...] = jnp.zeros_like(acc)

        @pl.loop(0, 4)
        def _(q):
            left = w1[:, :, :, :, pl.ds(pl.multiple_of(q * 512, 512), 512)].reshape(512, 512)
            hidden = jnp.dot(comb[...], left, preferred_element_type=F32)
            hidden = jnp.maximum(hidden, 0.0).astype(BF)
            acc[...] += jnp.dot(hidden, w2[q].reshape(512, 512), preferred_element_type=F32)

        out_ref[...] = acc[...].astype(BF)

    s_start()
    flags_z()
    w_own()
    w_x_own()
    f_own()
    pick(0)
    y_send(0)
    w1[x, h, c] = w1_in[...]
    w2[x, h, c] = w2_in[...]
    s_mask()
    s_x1()
    flags_y()
    w_x_relay(0, h)
    s_x2()
    chain_near(0)
    prepare()
    y_relay(0)
    s_z1()
    f_relay(1)
    pick(1)
    y_send(1)
    chain_near(1)
    s_z2()
    w_x_done(0, h)
    chain_near(2)
    y_relay(1)
    s_z3()
    f_relay(2)
    pick(2)
    y_send(2)
    flags_done()
    degrees()
    y_done(0)
    sparse(0)
    chain_near(3)
    w_x(1, h_l)
    w_x(2, h_r)
    s_z4()
    chain_far(0)
    y_relay(2)
    f_relay(3)
    pick(3)
    y_send(3)
    chain_far(1)
    s_x3()
    w_x_relay(1, h_l)
    w_x_relay(2, h_r)
    chain_far(2)
    y_done(1)
    sparse(1)
    s_x4()
    chain_far(3)
    w_x(3, h_o)
    w_x_done(1, h_l)
    w_x_done(2, h_r)
    s_swap()
    w_x_relay(3, h_o)
    y_relay(3)
    y_done(2)
    sparse(2)
    w_x_done(3, h_o)
    s_done()
    dense_part()
    y_done(3)
    sparse(3)
    combine()
    for group, hh in enumerate((h, h_l, h_r, h_o)):
        w_core(group, hh)
    mlp()
    for copy, cond in pending:
        if cond is None:
            copy().wait_send()
        else:
            pl.when(cond)(lambda copy=copy: copy().wait_send())


def shards(features, stripe_owner, dense_weight, sparse_weight, send_blocks, target_block, first_weight, second_weight):
    flags = jnp.pad((send_blocks[0].T + 1).astype(F32), ((0, 6), (0, 112)))
    smem = pl.BlockSpec(memory_space=pltpu.SMEM)
    vmem = pl.BlockSpec(memory_space=pltpu.VMEM)
    hbm = pl.BlockSpec(memory_space=pl.ANY)
    return pl.pallas_call(
        kernel,
        out_shape=jax.ShapeDtypeStruct((512, 512), BF),
        in_specs=[smem, smem, vmem, vmem, vmem, vmem, hbm, hbm],
        out_specs=vmem,
        scratch_shapes=[
            pltpu.VMEM((4, 512, 512), BF),
            pltpu.VMEM((16, 8, 128), F32),
            pltpu.VMEM((32, 16, 128), BF),
            pltpu.VMEM((4, 3, 2, 128, 512), BF),
            pltpu.VMEM((4, 2, 128, 512), BF),
            pltpu.VMEM((16, 2, 128, 512), BF),
            pltpu.VMEM((16, 512, 256), BF),
            pltpu.VMEM((4, 4, 2, 16, 2048), BF),
            pltpu.VMEM((4, 4, 2, 64, 512), BF),
            pltpu.VMEM((512, 512), BF),
            pltpu.VMEM((4, 128, 512), BF),
            pltpu.VMEM((2, 64, 512), BF),
            pltpu.VMEM((2, 128, 512), BF),
            pltpu.VMEM((4, 32, 512), BF),
            pltpu.VMEM((2, 16, 512), BF),
            pltpu.VMEM((2, 32, 512), BF),
            pltpu.VMEM((2, 4, 4, 32, 512), BF),
            pltpu.VMEM((512, 1024), jnp.int32),
            pltpu.VMEM((16, 128, 128), jnp.int32),
            pltpu.VMEM((512, 1024), BF),
            pltpu.VMEM((512, 512), F32),
            pltpu.VMEM((512, 128), F32),
            pltpu.VMEM((512, 512), BF),
            pltpu.SemaphoreType.DMA((N_SEND,)),
            pltpu.SemaphoreType.DMA((N_RECV,)),
            pltpu.SemaphoreType.DMA((2,)),
        ],
        compiler_params=pltpu.CompilerParams(
            collective_id=0, has_side_effects=True, vmem_limit_bytes=56 * 2**20
        ),
    )(stripe_owner.T, target_block[0].T, features, flags, first_weight, second_weight, dense_weight, sparse_weight[0])


def solution(mesh):
    placed = (
        P(("wide", "narrow"), None),
        P(),
        P(("wide", "narrow"), None),
        P(("wide", "narrow"), None, None, None),
        P(("wide", "narrow"), None, None),
        P(("wide", "narrow"), None, None),
        P("wide", None),
        P("wide", None),
    )
    return jax.shard_map(
        shards, mesh=mesh, in_specs=placed, out_specs=P(("wide", "narrow"), None), check_vma=False
    )
```

```python
import jax
import jax.numpy as jnp
from jax import lax
from jax.experimental import pallas as pl
from jax.experimental.pallas import tpu as pltpu
from jax.sharding import PartitionSpec as P

MESH = pl.DeviceIdType.MESH
BF = jnp.bfloat16
F32 = jnp.float32
N_SEND = 192
N_RECV = 128


def kernel(
    owner_ref, target_ref, f_ref, list_ref, w1_in, w2_in, dense_hbm, tile_hbm, out_ref,
    zf, fl, gate, tx, got_x, route, w1, w2, partner_f, cand, rxh, rxp, candz, rzh, rzp,
    stripes, dense, tiles, dense16, acc, deg, comb, send_sem, recv_sem, load_sem,
):
    w, n = lax.axis_index("wide"), lax.axis_index("narrow")
    x, h, c = lax.div(w, 8), lax.rem(lax.div(w, 2), 4), lax.rem(w, 2)
    y, i = lax.div(n, 4), lax.rem(n, 4)

    def up(v, by=1):
        return lax.rem(v + by, 4)

    def at(xx=x, hh=h, cc=c, yy=y, ii=i):
        return {"wide": xx * 8 + hh * 2 + cc, "narrow": yy * 4 + ii}

    x_r, x_l, x_o = up(x), up(x, 3), up(x, 2)
    h_r, h_l, h_o = up(h), up(h, 3), up(h, 2)
    y_r, y_l, y_o = up(y), up(y, 3), up(y, 2)
    right_x, left_x = at(xx=x_r), at(xx=x_l)
    right_h, left_h = at(hh=h_r), at(hh=h_l)
    right_y, left_y, far_y = at(yy=y_r), at(yy=y_l), at(yy=y_o)
    partner = at(cc=1 - c)
    right_z, left_z = at(ii=up(i)), at(ii=up(i, 3))
    low_end, high_end = i == 0, i == 3
    end, middle = low_end | high_end, (i == 1) | (i == 2)
    line = [at(ii=up(i, k)) for k in (1, 2, 3)]

    pending = []
    count = {"send": 0, "recv": 0}

    def slots(kind, k=1):
        count[kind] += k
        return count[kind] - k

    def send(src, dst, recv, device, cond=None):
        slot = slots("send")

        def copy():
            return pltpu.make_async_remote_copy(
                src_ref=src, dst_ref=dst, send_sem=send_sem.at[slot], recv_sem=recv_sem.at[recv],
                device_id=device, device_id_type=MESH,
            )

        if cond is None:
            copy().start()
        else:
            pl.when(cond)(lambda: copy().start())
        pending.append((copy, cond))

    def send_apart(src, dst, cut, recv, device, cond=None):
        slot = slots("send")
        size = src.shape[0]

        def copy(lo, hi):
            part = pl.ds(lo, hi - lo)
            return pltpu.make_async_remote_copy(
                src_ref=src.at[part], dst_ref=dst.at[part], send_sem=send_sem.at[slot], recv_sem=recv_sem.at[recv],
                device_id=device, device_id_type=MESH,
            )

        def start():
            @pl.when(c == 0)
            def _():
                copy(0, size).start()

            @pl.when(c == 1)
            def _():
                copy(0, cut).start()
                copy(cut, size).start()

        if cond is None:
            start()
        else:
            pl.when(cond)(start)
        pending.append((lambda: copy(0, size), cond))

    def arrived(dst, recv):
        pltpu.make_async_remote_copy(
            src_ref=dst, dst_ref=dst, send_sem=send_sem.at[0], recv_sem=recv_sem.at[recv],
            device_id=partner, device_id_type=MESH,
        ).wait_recv()

    loads = [
        pltpu.make_async_copy(dense_hbm, dense, load_sem.at[0]),
        pltpu.make_async_copy(tile_hbm, tiles, load_sem.at[1]),
    ]
    for load in loads:
        load.start()
    barrier = pltpu.get_barrier_semaphore()
    peers = [right_x, left_x, right_h, left_h, right_y, left_y, far_y, partner, *line]
    for peer in [*peers, at(hh=h_l, ii=3), at(hh=h_r, ii=0)]:
        pl.semaphore_signal(barrier, inc=1, device_id=peer, device_id_type=MESH)
    fl[n] = jnp.zeros((8, 128), F32)
    fl[n, 0:2, 0:16] = (list_ref[...] + 1).astype(F32)
    acc[...] = jnp.zeros_like(acc)
    pl.semaphore_wait(barrier, len(peers) + jnp.where(end, 4, 0))

    r_flag = slots("recv", 4)
    r_flag_y = slots("recv", 4)
    r_f = slots("recv", 8)
    r_part = slots("recv")
    r_swap = slots("recv")
    r_y = slots("recv", 32)
    r_chain = slots("recv", 6)
    r_wx = slots("recv", 24)
    r_wc = slots("recv", 8)
    r_s = slots("recv", 16)

    def w_near(to_right, to_left, away):
        own = ((w1_in, w1), (w2_in, w2))
        for part in to_right:
            send(own[part][0], own[part][1].at[x, h, c], r_chain + part, at(hh=h_r, ii=away), high_end)
        for part in to_left:
            send(own[part][0], own[part][1].at[x, h, c], r_chain + 2 + part, at(hh=h_l, ii=3 - away), low_end)

    def w_far(away):
        send(w1.at[x, h_l, c], w1.at[x, h_l, c], r_chain + 4, at(hh=h_r, ii=away), high_end)
        send(w2.at[x, h_r, c], w2.at[x, h_r, c], r_chain + 5, at(hh=h_l, ii=3 - away), low_end)

    def w_far_got():
        @pl.when(high_end)
        def _():
            arrived(w1.at[x, h_l, c], r_chain + 0)

        @pl.when(low_end)
        def _():
            arrived(w2.at[x, h_r, c], r_chain + 3)

    lower = i < 2
    h_a, h_b = jnp.where(lower, h_l, h_r), jnp.where(lower, h_r, h_l)

    def w_a_done():
        arrived(w1.at[x, h_a, c], r_chain + jnp.where(lower, 0, 2))
        arrived(w2.at[x, h_a, c], r_chain + jnp.where(lower, 1, 3))

    def w_b_done():
        @pl.when(jnp.logical_not(high_end))
        def _():
            arrived(w1.at[x, h_b, c], r_chain + jnp.where(lower, 2, 0))

        @pl.when(jnp.logical_not(low_end))
        def _():
            arrived(w2.at[x, h_b, c], r_chain + jnp.where(lower, 3, 1))

    def w_far_done():
        arrived(w1.at[x, h_o, c], r_chain + 4)
        arrived(w2.at[x, h_o, c], r_chain + 5)

    def w_x_own():
        for part, (src, buf) in enumerate(((w1_in, w1), (w2_in, w2))):
            send(src, buf.at[x, h, c], r_wx + part, right_x)
            send(src, buf.at[x, h, c], r_wx + 2 + part, left_x)

    def w_x(group, hh):
        base = r_wx + 6 * group
        for part, buf in enumerate((w1, w2)):
            send(buf.at[x, hh, c], buf.at[x, hh, c], base + part, right_x)
            send(buf.at[x, hh, c], buf.at[x, hh, c], base + 2 + part, left_x)

    def w_x_relay(group, hh):
        base = r_wx + 6 * group
        arrived(w1.at[x_l, hh, c], base + 0)
        send(w1.at[x_l, hh, c], w1.at[x_l, hh, c], base + 4, right_x)
        arrived(w2.at[x_r, hh, c], base + 3)
        send(w2.at[x_r, hh, c], w2.at[x_r, hh, c], base + 5, left_x)

    def w_x_done(group, hh):
        base = r_wx + 6 * group
        arrived(w2.at[x_l, hh, c], base + 1)
        arrived(w1.at[x_r, hh, c], base + 2)
        arrived(w1.at[x_o, hh, c], base + 4)
        arrived(w2.at[x_o, hh, c], base + 5)
        send(w1.at[:, hh, c], w1.at[:, hh, c], r_wc + 2 * group, partner)
        send(w2.at[:, hh, c], w2.at[:, hh, c], r_wc + 2 * group + 1, partner)

    def w_core(group, hh):
        arrived(w1.at[:, hh, 1 - c], r_wc + 2 * group)
        arrived(w2.at[:, hh, 1 - c], r_wc + 2 * group + 1)

    def s_start():
        send(f_ref, partner_f, r_part, partner)

    def s_mask():
        owner = owner_ref[c, n]
        mine = jnp.where(owner == w, 1.0, 0.0)
        other = jnp.where(owner == w + 1 - 2 * c, 1.0, 0.0)
        arrived(partner_f, r_part)
        for q in range(4):
            rows = pl.ds(q * 128, 128)
            cand[q] = (f_ref[rows, :].astype(F32) * mine + partner_f[rows, :].astype(F32) * other).astype(BF)

    def rs_first(buf, half, me_o, rbuf, base, right, left):
        send(buf.at[me_o, pl.ds(0, half)], rbuf.at[0], base + 0, right)
        send(buf.at[me_o, pl.ds(half, half)], rbuf.at[1], base + 1, left)

    def rs_second(buf, half, me_r, me_l, rbuf, pbuf, base, right, left):
        arrived(rbuf.at[0], base + 0)
        buf[me_r, 0:half] = buf[me_r, 0:half] + rbuf[0]
        arrived(rbuf.at[1], base + 1)
        buf[me_l, half:] = buf[me_l, half:] + rbuf[1]
        send(buf.at[me_r], pbuf.at[0], base + 2, right)
        send(buf.at[me_l], pbuf.at[1], base + 3, left)

    def s_x1():
        rs_first(cand, 64, x_o, rxh, r_s + 0, right_x, left_x)

    def s_x2():
        rs_second(cand, 64, x_r, x_l, rxh, rxp, r_s + 0, right_x, left_x)

    def s_z1():
        arrived(rxp.at[0], r_s + 2)
        arrived(rxp.at[1], r_s + 3)
        candz[...] = (cand[x] + rxp[0] + rxp[1]).reshape(4, 32, 512)
        rs_first(candz, 16, h_o, rzh, r_s + 4, right_h, left_h)

    def s_z2():
        rs_second(candz, 16, h_r, h_l, rzh, rzp, r_s + 4, right_h, left_h)

    def s_z3():
        arrived(rzp.at[0], r_s + 6)
        arrived(rzp.at[1], r_s + 7)
        stripes[c, x, h] = candz[h] + rzp[0] + rzp[1]
        piece = stripes.at[c, x, h]
        send(piece, piece, r_s + 8, right_h)
        send(piece, piece, r_s + 9, left_h)

    def s_z4():
        arrived(stripes.at[c, x, h_l], r_s + 8)
        half = stripes.at[c, x, h_l, pl.ds(0, 16)]
        send(half, half, r_s + 10, right_h)
        arrived(stripes.at[c, x, h_r], r_s + 9)
        half = stripes.at[c, x, h_r, pl.ds(16, 16)]
        send(half, half, r_s + 11, left_h)

    def s_x3():
        arrived(stripes.at[c, x, h_o, pl.ds(0, 16)], r_s + 10)
        arrived(stripes.at[c, x, h_o, pl.ds(16, 16)], r_s + 11)
        piece = stripes.at[c, x]
        send(piece, piece, r_s + 12, right_x)
        send(piece, piece, r_s + 13, left_x)

    def s_x4():
        arrived(stripes.at[c, x_l], r_s + 12)
        half = stripes.at[c, x_l, pl.ds(0, 2)]
        send(half, half, r_s + 14, right_x)
        arrived(stripes.at[c, x_r], r_s + 13)
        half = stripes.at[c, x_r, pl.ds(2, 2)]
        send(half, half, r_s + 15, left_x)

    def s_swap():
        arrived(stripes.at[c, x_o, pl.ds(0, 2)], r_s + 14)
        arrived(stripes.at[c, x_o, pl.ds(2, 2)], r_s + 15)
        send(stripes.at[c], stripes.at[c], r_swap, partner)

    def s_done():
        arrived(stripes.at[1 - c], r_swap)

    def flags_z():
        for k in (1, 2, 3):
            send(fl.at[n], fl.at[n], r_flag + i, line[k - 1])

    def flags_y():
        for k in (1, 2, 3):
            j = up(i, k)
            arrived(fl.at[y * 4 + j], r_flag + j)
        row = fl.at[pl.ds(y * 4, 4)]
        for device in (right_y, left_y, far_y):
            send(row, row, r_flag_y + y, device)

    def flags_done():
        for k in (1, 2, 3):
            yy = up(y, k)
            arrived(fl.at[pl.ds(yy * 4, 4)], r_flag_y + yy)

    first = jnp.where(i == 0, 1, i - 1)
    second = jnp.where(i == 0, 2, jnp.where(i == 1, 2, jnp.where(i == 2, 3, 1)))
    third = jnp.where(i < 2, 3, 0)
    order = [i, first, second, third]

    def f_own(half):
        source = f_ref.at[:, pl.ds(half * 256, 256)]
        send(source, zf.at[i, half], r_f + i * 2 + half, right_z, i < 3)
        send(source, zf.at[i, half], r_f + i * 2 + half, left_z, i > 0)

    def f_got(k, half, cond=None):
        def wait():
            arrived(zf.at[order[k], half], r_f + order[k] * 2 + half)

        if cond is None:
            wait()
        else:
            pl.when(cond)(wait)

    def f_relay(k, half):
        j = order[k]
        send(zf.at[j, half], zf.at[j, half], r_f + j * 2 + half, right_z, (j < i) & (i < 3))
        send(zf.at[j, half], zf.at[j, half], r_f + j * 2 + half, left_z, (j > i) & (i > 0))

    def gates(k):
        tile = fl[y * 4 + order[k]]
        lane = lax.broadcasted_iota(jnp.int32, (8, 128), 1)
        for d in range(4):
            column = up(y, d) * 4 + i
            value = jnp.sum(jnp.where(lane == column, tile, 0.0), axis=1, keepdims=True)
            for s in range(2):
                one = jnp.broadcast_to(value[s : s + 1, :], (16, 128))
                for e in range(4):
                    gate[(d * 2 + s) * 4 + e] = jnp.where(one == e + 1.0, 1.0, 0.0).astype(BF)

    def pick(k, half):
        j = order[k]

        @pl.loop(0, 8)
        def _(r):
            blocks = []
            for e in range(4):
                rows = pl.ds(pl.multiple_of(e * 128 + r * 16, 16), 16)
                blocks.append(f_ref[rows, half * 256 : half * 256 + 256] if k == 0 else zf[j, half, rows, :])
            rows = pl.ds(pl.multiple_of(r * 16, 16), 16)
            for d in range(4):
                for s in range(2):
                    total = None
                    for e in range(4):
                        g = gate[(d * 2 + s) * 4 + e]
                        term = blocks[e] * jnp.concatenate([g, g], axis=1)
                        total = term if total is None else total + term
                    if d == 0:
                        got_x[k, half, 0, s, rows, :] = total
                    elif d == 2:
                        tx[k, half, s, 2, rows, :] = total
                    else:
                        tx[k, half, d // 2, s, rows, :] = total

    def y_send(k, half):
        base = r_y + 8 * k + 4 * half
        for way, device in enumerate((right_y, left_y)):
            if k == 0 and half == 0:
                send_apart(tx.at[k, half, way], got_x.at[k, half, 1 + way], 1, base + way, device)
            else:
                send(tx.at[k, half, way], got_x.at[k, half, 1 + way], base + way, device)

    def y_relay(k, half):
        base = r_y + 8 * k + 4 * half
        for way, device in enumerate((right_y, left_y)):
            arrived(got_x.at[k, half, 1 + way], base + way)
            send(got_x.at[k, half, 1 + way, 2], got_x.at[k, half, 3, way], base + 2 + way, device)

    def y_done(k, half):
        base = r_y + 8 * k + 4 * half
        arrived(got_x.at[k, half, 3, 0], base + 2)
        arrived(got_x.at[k, half, 3, 1], base + 3)

    def prepare():
        for load in loads:
            load.wait()
        for q in range(4):
            rows = pl.ds(q * 128, 128)
            block = dense[rows, :]
            dense16[rows, :] = block.astype(F32).astype(BF)
            total = 1.0 + jnp.sum(block.astype(F32), axis=1, keepdims=True)
            deg[rows, :] = jnp.broadcast_to(total, (128, 128))

        @pl.loop(0, 16)
        def _(p):
            tile = tiles[p].astype(F32)
            for s in range(2):
                for b in range(4):
                    hit = jnp.where(target_ref[s, p] == b, 1.0, 0.0)
                    route[p, pl.ds(b * 128, 128), pl.ds(s * 128, 128)] = (tile * hit).astype(BF)

    def sparse(k, half, low=0, high=4):
        columns = slice(half * 256, half * 256 + 256)

        @pl.loop(low, high)
        def _(source):
            away = jnp.where(source == 1, 3, jnp.where(source == 2, 1, jnp.where(source == 3, 2, 0)))
            p = lax.rem(y + away, 4) * 4 + order[k]
            block = got_x[k, half, source, 0:2].reshape(256, 256)
            acc[:, columns] += jnp.dot(route[p], block, preferred_element_type=F32)

    def degrees(k):
        @pl.loop(0, 4)
        def _(yy):
            p = yy * 4 + order[k]
            lane = lax.broadcasted_iota(jnp.int32, (8, 128), 1)
            value = jnp.sum(jnp.where(lane == n, fl[p], 0.0), axis=1, keepdims=True)
            present = jnp.minimum(value, 1.0)
            ones = [jnp.broadcast_to(present[s : s + 1, :], (128, 128)) for s in range(2)]
            ones = jnp.concatenate(ones, axis=0).astype(BF)
            deg[...] += jnp.dot(route[p], ones, preferred_element_type=F32)

    def dense_part():
        for k in range(2):
            block = stripes[k].reshape(512, 512)
            acc[...] += jnp.dot(dense16[:, k * 512 : (k + 1) * 512], block, preferred_element_type=F32)

    def combine():
        for q in range(4):
            rows = pl.ds(q * 128, 128)
            scale = 1.0 / jnp.sqrt(deg[rows, :])
            scale = jnp.concatenate([scale, scale, scale, scale], axis=1)
            comb[rows, :] = (f_ref[rows, :].astype(F32) + acc[rows, :] * scale).astype(BF)

    def mlp():
        acc[...] = jnp.zeros_like(acc)

        @pl.loop(0, 4)
        def _(q):
            left = w1[:, :, :, :, pl.ds(pl.multiple_of(q * 512, 512), 512)].reshape(512, 512)
            hidden = jnp.dot(comb[...], left, preferred_element_type=F32)
            hidden = jnp.maximum(hidden, 0.0).astype(BF)
            acc[...] += jnp.dot(hidden, w2[q].reshape(512, 512), preferred_element_type=F32)

        out_ref[...] = acc[...].astype(BF)

    both = (0, 1)
    s_start()
    flags_z()
    f_own(0)
    f_own(1)
    w_near((0,), (1,), 3)
    w_near(both, both, 0)
    gates(0)
    pick(0, 0)
    y_send(0, 0)
    pick(0, 1)
    y_send(0, 1)
    s_mask()
    s_x1()
    w_x_own()
    w1[x, h, c] = w1_in[...]
    w2[x, h, c] = w2_in[...]
    flags_y()
    s_x2()
    prepare()
    f_got(1, 0)
    f_got(2, 0, middle)
    gates(1)
    pick(1, 0)
    s_z1()
    f_relay(1, 0)
    f_relay(2, 0)
    y_relay(0, 0)
    y_send(1, 0)
    w_far_got()
    w_far(0)
    w_near(both, both, 1)
    w_far(1)
    f_got(1, 1)
    f_got(2, 1, middle)
    pick(1, 1)
    w_x_relay(0, h)
    s_z2()
    f_relay(1, 1)
    f_relay(2, 1)
    y_relay(0, 1)
    y_send(1, 1)
    f_got(2, 0, end)
    f_got(3, 0, middle)
    gates(2)
    pick(2, 0)
    s_z3()
    f_relay(3, 0)
    y_relay(1, 0)
    y_send(2, 0)
    w_near(both, both, 2)
    w_far(2)
    w_a_done()
    w_x(1, h_a)
    w_x_done(0, h)
    f_got(2, 1, end)
    f_got(3, 1, middle)
    pick(2, 1)
    s_z4()
    f_relay(3, 1)
    y_relay(1, 1)
    y_send(2, 1)
    flags_done()
    for k in range(4):
        degrees(k)
    y_done(0, 0)
    y_done(0, 1)
    sparse(0, 0)
    sparse(0, 1)
    w_x_relay(1, h_a)
    f_got(3, 0, end)
    gates(3)
    pick(3, 0)
    y_relay(2, 0)
    y_send(3, 0)
    w_near((1,), (0,), 3)
    w_far(3)
    s_x3()
    f_got(3, 1, end)
    pick(3, 1)
    y_relay(2, 1)
    y_send(3, 1)
    y_done(1, 0)
    y_done(1, 1)
    sparse(1, 0)
    sparse(1, 1)
    s_x4()
    w_b_done()
    w_x(2, h_b)
    w_far_done()
    w_x(3, h_o)
    w_x_done(1, h_a)
    s_swap()
    y_relay(3, 0)
    w_x_relay(2, h_b)
    w_x_relay(3, h_o)
    y_done(2, 0)
    y_done(2, 1)
    sparse(2, 0)
    sparse(2, 1)
    w_x_done(2, h_b)
    y_relay(3, 1)
    w_x_done(3, h_o)
    sparse(3, 0, 0, 3)
    s_done()
    dense_part()
    sparse(3, 1, 0, 3)
    y_done(3, 0)
    sparse(3, 0, 3, 4)
    y_done(3, 1)
    sparse(3, 1, 3, 4)
    combine()
    for group, hh in enumerate((h, h_a, h_b, h_o)):
        w_core(group, hh)
    mlp()
    for copy, cond in pending:
        if cond is None:
            copy().wait_send()
        else:
            pl.when(cond)(lambda copy=copy: copy().wait_send())


def shards(features, stripe_owner, dense_weight, sparse_weight, send_blocks, target_block, first_weight, second_weight):
    smem = pl.BlockSpec(memory_space=pltpu.SMEM)
    vmem = pl.BlockSpec(memory_space=pltpu.VMEM)
    hbm = pl.BlockSpec(memory_space=pl.ANY)
    return pl.pallas_call(
        kernel,
        out_shape=jax.ShapeDtypeStruct((512, 512), BF),
        in_specs=[smem, smem, vmem, vmem, vmem, vmem, hbm, hbm],
        out_specs=vmem,
        scratch_shapes=[
            pltpu.VMEM((4, 2, 512, 256), BF),
            pltpu.VMEM((16, 8, 128), F32),
            pltpu.VMEM((32, 16, 128), BF),
            pltpu.VMEM((4, 2, 2, 3, 128, 256), BF),
            pltpu.VMEM((4, 2, 4, 3, 128, 256), BF),
            pltpu.VMEM((16, 512, 256), BF),
            pltpu.VMEM((4, 4, 2, 16, 2048), BF),
            pltpu.VMEM((4, 4, 2, 64, 512), BF),
            pltpu.VMEM((512, 512), BF),
            pltpu.VMEM((4, 128, 512), BF),
            pltpu.VMEM((2, 64, 512), BF),
            pltpu.VMEM((2, 128, 512), BF),
            pltpu.VMEM((4, 32, 512), BF),
            pltpu.VMEM((2, 16, 512), BF),
            pltpu.VMEM((2, 32, 512), BF),
            pltpu.VMEM((2, 4, 4, 32, 512), BF),
            pltpu.VMEM((512, 1024), jnp.int32),
            pltpu.VMEM((16, 128, 128), jnp.int32),
            pltpu.VMEM((512, 1024), BF),
            pltpu.VMEM((512, 512), F32),
            pltpu.VMEM((512, 128), F32),
            pltpu.VMEM((512, 512), BF),
            pltpu.SemaphoreType.DMA((N_SEND,)),
            pltpu.SemaphoreType.DMA((N_RECV,)),
            pltpu.SemaphoreType.DMA((2,)),
        ],
        compiler_params=pltpu.CompilerParams(
            collective_id=0, has_side_effects=True, vmem_limit_bytes=56 * 2**20
        ),
    )(stripe_owner.T, target_block[0].T, features, send_blocks[0].T, first_weight, second_weight, dense_weight, sparse_weight[0])


def solution(mesh):
    placed = (
        P(("wide", "narrow"), None),
        P(),
        P(("wide", "narrow"), None),
        P(("wide", "narrow"), None, None, None),
        P(("wide", "narrow"), None, None),
        P(("wide", "narrow"), None, None),
        P("wide", None),
        P("wide", None),
    )
    return jax.shard_map(
        shards, mesh=mesh, in_specs=placed, out_specs=P(("wide", "narrow"), None), check_vma=False
    )
```

```python
import jax
import jax.numpy as jnp
from jax import lax
from jax.experimental import pallas as pl
from jax.experimental.pallas import tpu as pltpu
from jax.sharding import PartitionSpec as P

MESH = pl.DeviceIdType.MESH
BF = jnp.bfloat16
F32 = jnp.float32
N_SEND = 192
N_RECV = 128


def kernel(
    owner_ref, target_ref, f_ref, list_ref, w1_in, w2_in, dense_hbm, tile_hbm, out_ref,
    zf, fl, gate, tx, got_x, route, w1, w2, partner_f, cand, rxh, rxp, candz, rzh, rzp,
    stripes, dense, tiles, dense16, acc, deg, comb, send_sem, recv_sem, load_sem,
):
    w, n = lax.axis_index("wide"), lax.axis_index("narrow")
    x, h, c = lax.div(w, 8), lax.rem(lax.div(w, 2), 4), lax.rem(w, 2)
    y, i = lax.div(n, 4), lax.rem(n, 4)

    def up(v, by=1):
        return lax.rem(v + by, 4)

    def at(xx=x, hh=h, cc=c, yy=y, ii=i):
        return {"wide": xx * 8 + hh * 2 + cc, "narrow": yy * 4 + ii}

    x_r, x_l, x_o = up(x), up(x, 3), up(x, 2)
    h_r, h_l, h_o = up(h), up(h, 3), up(h, 2)
    y_r, y_l, y_o = up(y), up(y, 3), up(y, 2)
    right_x, left_x = at(xx=x_r), at(xx=x_l)
    right_h, left_h = at(hh=h_r), at(hh=h_l)
    right_y, left_y, far_y = at(yy=y_r), at(yy=y_l), at(yy=y_o)
    partner = at(cc=1 - c)
    right_z, left_z = at(ii=up(i)), at(ii=up(i, 3))
    low_end, high_end = i == 0, i == 3
    end, middle = low_end | high_end, (i == 1) | (i == 2)
    line = [at(ii=up(i, k)) for k in (1, 2, 3)]

    pending = []
    count = {"send": 0, "recv": 0}

    def slots(kind, k=1):
        count[kind] += k
        return count[kind] - k

    def send(src, dst, recv, device, cond=None):
        slot = slots("send")

        def copy():
            return pltpu.make_async_remote_copy(
                src_ref=src, dst_ref=dst, send_sem=send_sem.at[slot], recv_sem=recv_sem.at[recv],
                device_id=device, device_id_type=MESH,
            )

        if cond is None:
            copy().start()
        else:
            pl.when(cond)(lambda: copy().start())
        pending.append((copy, cond))

    def send_apart(src, dst, cut, recv, device, cond=None):
        slot = slots("send")
        size = src.shape[0]

        def copy(lo, hi):
            part = pl.ds(lo, hi - lo)
            return pltpu.make_async_remote_copy(
                src_ref=src.at[part], dst_ref=dst.at[part], send_sem=send_sem.at[slot], recv_sem=recv_sem.at[recv],
                device_id=device, device_id_type=MESH,
            )

        def start():
            @pl.when(c == 0)
            def _():
                copy(0, size).start()

            @pl.when(c == 1)
            def _():
                copy(0, cut).start()
                copy(cut, size).start()

        if cond is None:
            start()
        else:
            pl.when(cond)(start)
        pending.append((lambda: copy(0, size), cond))

    def arrived(dst, recv):
        pltpu.make_async_remote_copy(
            src_ref=dst, dst_ref=dst, send_sem=send_sem.at[0], recv_sem=recv_sem.at[recv],
            device_id=partner, device_id_type=MESH,
        ).wait_recv()

    loads = [
        pltpu.make_async_copy(dense_hbm, dense, load_sem.at[0]),
        pltpu.make_async_copy(tile_hbm, tiles, load_sem.at[1]),
    ]
    for load in loads:
        load.start()
    barrier = pltpu.get_barrier_semaphore()
    peers = [right_x, left_x, right_h, left_h, right_y, left_y, far_y, partner, *line]
    for peer in [*peers, at(hh=h_l, ii=3), at(hh=h_r, ii=0)]:
        pl.semaphore_signal(barrier, inc=1, device_id=peer, device_id_type=MESH)
    fl[n] = jnp.zeros((8, 128), F32)
    fl[n, 0:2, 0:16] = (list_ref[...] + 1).astype(F32)
    acc[...] = jnp.zeros_like(acc)
    pl.semaphore_wait(barrier, len(peers) + jnp.where(end, 4, 0))

    r_flag = slots("recv", 4)
    r_flag_y = slots("recv", 4)
    r_f = slots("recv", 8)
    r_part = slots("recv")
    r_swap = slots("recv", 4)
    r_y = slots("recv", 32)
    r_chain = slots("recv", 6)
    r_wx = slots("recv", 24)
    r_wc = slots("recv", 8)
    r_s = slots("recv", 16)

    def w_near(to_right, to_left, away):
        own = ((w1_in, w1), (w2_in, w2))
        for part in to_right:
            send(own[part][0], own[part][1].at[x, h, c], r_chain + part, at(hh=h_r, ii=away), high_end)
        for part in to_left:
            send(own[part][0], own[part][1].at[x, h, c], r_chain + 2 + part, at(hh=h_l, ii=3 - away), low_end)

    def w_far(away):
        send(w1.at[x, h_l, c], w1.at[x, h_l, c], r_chain + 4, at(hh=h_r, ii=away), high_end)
        send(w2.at[x, h_r, c], w2.at[x, h_r, c], r_chain + 5, at(hh=h_l, ii=3 - away), low_end)

    def w_far_got():
        @pl.when(high_end)
        def _():
            arrived(w1.at[x, h_l, c], r_chain + 0)

        @pl.when(low_end)
        def _():
            arrived(w2.at[x, h_r, c], r_chain + 3)

    lower = i < 2
    h_a, h_b = jnp.where(lower, h_l, h_r), jnp.where(lower, h_r, h_l)

    def w_a_done():
        arrived(w1.at[x, h_a, c], r_chain + jnp.where(lower, 0, 2))
        arrived(w2.at[x, h_a, c], r_chain + jnp.where(lower, 1, 3))

    def w_b_done():
        @pl.when(jnp.logical_not(high_end))
        def _():
            arrived(w1.at[x, h_b, c], r_chain + jnp.where(lower, 2, 0))

        @pl.when(jnp.logical_not(low_end))
        def _():
            arrived(w2.at[x, h_b, c], r_chain + jnp.where(lower, 3, 1))

    def w_far_done():
        arrived(w1.at[x, h_o, c], r_chain + 4)
        arrived(w2.at[x, h_o, c], r_chain + 5)

    def w_x_own():
        for part, (src, buf) in enumerate(((w1_in, w1), (w2_in, w2))):
            send(src, buf.at[x, h, c], r_wx + part, right_x)
            send(src, buf.at[x, h, c], r_wx + 2 + part, left_x)

    def w_x(group, hh):
        base = r_wx + 6 * group
        for part, buf in enumerate((w1, w2)):
            send(buf.at[x, hh, c], buf.at[x, hh, c], base + part, right_x)
            send(buf.at[x, hh, c], buf.at[x, hh, c], base + 2 + part, left_x)

    def w_x_relay(group, hh):
        base = r_wx + 6 * group
        arrived(w1.at[x_l, hh, c], base + 0)
        send(w1.at[x_l, hh, c], w1.at[x_l, hh, c], base + 4, right_x)
        arrived(w2.at[x_r, hh, c], base + 3)
        send(w2.at[x_r, hh, c], w2.at[x_r, hh, c], base + 5, left_x)

    def w_x_done(group, hh):
        base = r_wx + 6 * group
        arrived(w2.at[x_l, hh, c], base + 1)
        arrived(w1.at[x_r, hh, c], base + 2)
        arrived(w1.at[x_o, hh, c], base + 4)
        arrived(w2.at[x_o, hh, c], base + 5)
        send(w1.at[:, hh, c], w1.at[:, hh, c], r_wc + 2 * group, partner)
        send(w2.at[:, hh, c], w2.at[:, hh, c], r_wc + 2 * group + 1, partner)

    def w_core(group, hh):
        arrived(w1.at[:, hh, 1 - c], r_wc + 2 * group)
        arrived(w2.at[:, hh, 1 - c], r_wc + 2 * group + 1)

    def s_start():
        send(f_ref, partner_f, r_part, partner)

    def s_mask():
        owner = owner_ref[c, n]
        mine = jnp.where(owner == w, 1.0, 0.0)
        other = jnp.where(owner == w + 1 - 2 * c, 1.0, 0.0)
        arrived(partner_f, r_part)
        for q in range(4):
            rows = pl.ds(q * 128, 128)
            cand[q] = (f_ref[rows, :].astype(F32) * mine + partner_f[rows, :].astype(F32) * other).astype(BF)

    def rs_first(buf, half, me_o, rbuf, base, right, left):
        send(buf.at[me_o, pl.ds(0, half)], rbuf.at[0], base + 0, right)
        send(buf.at[me_o, pl.ds(half, half)], rbuf.at[1], base + 1, left)

    def rs_second(buf, half, me_r, me_l, rbuf, pbuf, base, right, left):
        arrived(rbuf.at[0], base + 0)
        buf[me_r, 0:half] = buf[me_r, 0:half] + rbuf[0]
        arrived(rbuf.at[1], base + 1)
        buf[me_l, half:] = buf[me_l, half:] + rbuf[1]
        send(buf.at[me_r], pbuf.at[0], base + 2, right)
        send(buf.at[me_l], pbuf.at[1], base + 3, left)

    def s_x1():
        rs_first(cand, 64, x_o, rxh, r_s + 0, right_x, left_x)

    def s_x2():
        rs_second(cand, 64, x_r, x_l, rxh, rxp, r_s + 0, right_x, left_x)

    def s_z1():
        arrived(rxp.at[0], r_s + 2)
        arrived(rxp.at[1], r_s + 3)
        candz[...] = (cand[x] + rxp[0] + rxp[1]).reshape(4, 32, 512)
        rs_first(candz, 16, h_o, rzh, r_s + 4, right_h, left_h)

    def s_z2():
        rs_second(candz, 16, h_r, h_l, rzh, rzp, r_s + 4, right_h, left_h)

    def s_z3():
        arrived(rzp.at[0], r_s + 6)
        arrived(rzp.at[1], r_s + 7)
        stripes[c, x, h] = candz[h] + rzp[0] + rzp[1]
        piece = stripes.at[c, x, h]
        send(piece, piece, r_s + 8, right_h)
        send(piece, piece, r_s + 9, left_h)

    def s_z4():
        arrived(stripes.at[c, x, h_l], r_s + 8)
        half = stripes.at[c, x, h_l, pl.ds(0, 16)]
        send(half, half, r_s + 10, right_h)
        arrived(stripes.at[c, x, h_r], r_s + 9)
        half = stripes.at[c, x, h_r, pl.ds(16, 16)]
        send(half, half, r_s + 11, left_h)

    def s_x3():
        arrived(stripes.at[c, x, h_o, pl.ds(0, 16)], r_s + 10)
        arrived(stripes.at[c, x, h_o, pl.ds(16, 16)], r_s + 11)
        piece = stripes.at[c, x]
        send(piece, piece, r_s + 12, right_x)
        send(piece, piece, r_s + 13, left_x)
        send(piece, piece, r_swap + 0, partner)

    def s_x4():
        arrived(stripes.at[c, x_l], r_s + 12)
        half = stripes.at[c, x_l, pl.ds(0, 2)]
        send(half, half, r_s + 14, right_x)
        arrived(stripes.at[c, x_r], r_s + 13)
        half = stripes.at[c, x_r, pl.ds(2, 2)]
        send(half, half, r_s + 15, left_x)
        send(stripes.at[c, x_l], stripes.at[c, x_l], r_swap + 1, partner)
        send(stripes.at[c, x_r], stripes.at[c, x_r], r_swap + 2, partner)

    def s_swap():
        arrived(stripes.at[c, x_o, pl.ds(0, 2)], r_s + 14)
        arrived(stripes.at[c, x_o, pl.ds(2, 2)], r_s + 15)
        send(stripes.at[c, x_o], stripes.at[c, x_o], r_swap + 3, partner)

    def s_done():
        for k, xx in enumerate((x, x_l, x_r, x_o)):
            arrived(stripes.at[1 - c, xx], r_swap + k)

    def flags_z():
        for k in (1, 2, 3):
            send(fl.at[n], fl.at[n], r_flag + i, line[k - 1])

    def flags_y():
        for k in (1, 2, 3):
            j = up(i, k)
            arrived(fl.at[y * 4 + j], r_flag + j)
        row = fl.at[pl.ds(y * 4, 4)]
        for device in (right_y, left_y, far_y):
            send(row, row, r_flag_y + y, device)

    def flags_done():
        for k in (1, 2, 3):
            yy = up(y, k)
            arrived(fl.at[pl.ds(yy * 4, 4)], r_flag_y + yy)

    first = jnp.where(i == 0, 1, i - 1)
    second = jnp.where(i == 0, 2, jnp.where(i == 1, 2, jnp.where(i == 2, 3, 1)))
    third = jnp.where(i < 2, 3, 0)
    order = [i, first, second, third]

    def f_own(half):
        source = f_ref.at[:, pl.ds(half * 256, 256)]
        send(source, zf.at[i, half], r_f + i * 2 + half, right_z, i < 3)
        send(source, zf.at[i, half], r_f + i * 2 + half, left_z, i > 0)

    def f_got(k, half, cond=None):
        def wait():
            arrived(zf.at[order[k], half], r_f + order[k] * 2 + half)

        if cond is None:
            wait()
        else:
            pl.when(cond)(wait)

    def f_relay(k, half):
        j = order[k]
        send(zf.at[j, half], zf.at[j, half], r_f + j * 2 + half, right_z, (j < i) & (i < 3))
        send(zf.at[j, half], zf.at[j, half], r_f + j * 2 + half, left_z, (j > i) & (i > 0))

    def gates(k):
        tile = fl[y * 4 + order[k]]
        lane = lax.broadcasted_iota(jnp.int32, (8, 128), 1)
        for d in range(4):
            column = up(y, d) * 4 + i
            value = jnp.sum(jnp.where(lane == column, tile, 0.0), axis=1, keepdims=True)
            for s in range(2):
                one = jnp.broadcast_to(value[s : s + 1, :], (16, 128))
                for e in range(4):
                    gate[(d * 2 + s) * 4 + e] = jnp.where(one == e + 1.0, 1.0, 0.0).astype(BF)

    def pick(k, half):
        j = order[k]

        @pl.loop(0, 8)
        def _(r):
            blocks = []
            for e in range(4):
                rows = pl.ds(pl.multiple_of(e * 128 + r * 16, 16), 16)
                blocks.append(f_ref[rows, half * 256 : half * 256 + 256] if k == 0 else zf[j, half, rows, :])
            rows = pl.ds(pl.multiple_of(r * 16, 16), 16)
            for d in range(4):
                for s in range(2):
                    total = None
                    for e in range(4):
                        g = gate[(d * 2 + s) * 4 + e]
                        term = blocks[e] * jnp.concatenate([g, g], axis=1)
                        total = term if total is None else total + term
                    if d == 0:
                        got_x[k, half, 0, s, rows, :] = total
                    elif d == 2:
                        tx[k, half, s, 2, rows, :] = total
                    else:
                        tx[k, half, d // 2, s, rows, :] = total

    def y_send(k, half):
        base = r_y + 8 * k + 4 * half
        for way, device in enumerate((right_y, left_y)):
            if k == 0 and half == 0:
                send_apart(tx.at[k, half, way], got_x.at[k, half, 1 + way], 1, base + way, device)
            else:
                send(tx.at[k, half, way], got_x.at[k, half, 1 + way], base + way, device)

    def y_relay(k, half):
        base = r_y + 8 * k + 4 * half
        for way, device in enumerate((right_y, left_y)):
            arrived(got_x.at[k, half, 1 + way], base + way)
            send(got_x.at[k, half, 1 + way, 2], got_x.at[k, half, 3, way], base + 2 + way, device)

    def y_done(k, half):
        base = r_y + 8 * k + 4 * half
        arrived(got_x.at[k, half, 3, 0], base + 2)
        arrived(got_x.at[k, half, 3, 1], base + 3)

    def prepare():
        for load in loads:
            load.wait()
        for q in range(4):
            rows = pl.ds(q * 128, 128)
            block = dense[rows, :]
            dense16[rows, :] = block.astype(F32).astype(BF)
            total = 1.0 + jnp.sum(block.astype(F32), axis=1, keepdims=True)
            deg[rows, :] = jnp.broadcast_to(total, (128, 128))

        @pl.loop(0, 16)
        def _(p):
            tile = tiles[p].astype(F32)
            for s in range(2):
                for b in range(4):
                    hit = jnp.where(target_ref[s, p] == b, 1.0, 0.0)
                    route[p, pl.ds(b * 128, 128), pl.ds(s * 128, 128)] = (tile * hit).astype(BF)

    def sparse(k, half, low=0, high=4):
        columns = slice(half * 256, half * 256 + 256)

        @pl.loop(low, high)
        def _(source):
            away = jnp.where(source == 1, 3, jnp.where(source == 2, 1, jnp.where(source == 3, 2, 0)))
            p = lax.rem(y + away, 4) * 4 + order[k]
            block = got_x[k, half, source, 0:2].reshape(256, 256)
            acc[:, columns] += jnp.dot(route[p], block, preferred_element_type=F32)

    def degrees(k):
        @pl.loop(0, 4)
        def _(yy):
            p = yy * 4 + order[k]
            lane = lax.broadcasted_iota(jnp.int32, (8, 128), 1)
            value = jnp.sum(jnp.where(lane == n, fl[p], 0.0), axis=1, keepdims=True)
            present = jnp.minimum(value, 1.0)
            ones = [jnp.broadcast_to(present[s : s + 1, :], (128, 128)) for s in range(2)]
            ones = jnp.concatenate(ones, axis=0).astype(BF)
            deg[...] += jnp.dot(route[p], ones, preferred_element_type=F32)

    def dense_part():
        for k in range(2):
            block = stripes[k].reshape(512, 512)
            acc[...] += jnp.dot(dense16[:, k * 512 : (k + 1) * 512], block, preferred_element_type=F32)

    def combine():
        for q in range(4):
            rows = pl.ds(q * 128, 128)
            scale = 1.0 / jnp.sqrt(deg[rows, :])
            scale = jnp.concatenate([scale, scale, scale, scale], axis=1)
            comb[rows, :] = (f_ref[rows, :].astype(F32) + acc[rows, :] * scale).astype(BF)

    def mlp():
        acc[...] = jnp.zeros_like(acc)

        @pl.loop(0, 4)
        def _(q):
            left = w1[:, :, :, :, pl.ds(pl.multiple_of(q * 512, 512), 512)].reshape(512, 512)
            hidden = jnp.dot(comb[...], left, preferred_element_type=F32)
            hidden = jnp.maximum(hidden, 0.0).astype(BF)
            acc[...] += jnp.dot(hidden, w2[q].reshape(512, 512), preferred_element_type=F32)

        out_ref[...] = acc[...]

    both = (0, 1)
    s_start()
    flags_z()
    f_own(0)
    f_own(1)
    w_near((0,), (1,), 3)
    w_near(both, both, 0)
    gates(0)
    pick(0, 0)
    y_send(0, 0)
    pick(0, 1)
    y_send(0, 1)
    s_mask()
    s_x1()
    w_x_own()
    w1[x, h, c] = w1_in[...]
    w2[x, h, c] = w2_in[...]
    flags_y()
    s_x2()
    prepare()
    f_got(1, 0)
    f_got(2, 0, middle)
    gates(1)
    pick(1, 0)
    s_z1()
    f_relay(1, 0)
    f_relay(2, 0)
    y_relay(0, 0)
    y_send(1, 0)
    w_far_got()
    w_far(0)
    f_got(1, 1)
    f_got(2, 1, middle)
    pick(1, 1)
    w_x_relay(0, h)
    s_z2()
    f_relay(1, 1)
    f_relay(2, 1)
    y_relay(0, 1)
    y_send(1, 1)
    f_got(2, 0, end)
    f_got(3, 0, middle)
    gates(2)
    pick(2, 0)
    s_z3()
    f_relay(3, 0)
    y_relay(1, 0)
    y_send(2, 0)
    w_x_done(0, h)
    f_got(2, 1, end)
    f_got(3, 1, middle)
    pick(2, 1)
    s_z4()
    w_near(both, both, 1)
    w_far(1)
    w_near(both, both, 2)
    w_far(2)
    f_relay(3, 1)
    y_relay(1, 1)
    y_send(2, 1)
    flags_done()
    for k in range(4):
        degrees(k)
    y_done(0, 0)
    y_done(0, 1)
    sparse(0, 0)
    sparse(0, 1)
    f_got(3, 0, end)
    gates(3)
    pick(3, 0)
    y_relay(2, 0)
    y_send(3, 0)
    w_a_done()
    w_x(1, h_a)
    w_near((1,), (0,), 3)
    w_far(3)
    s_x3()
    f_got(3, 1, end)
    pick(3, 1)
    y_relay(2, 1)
    y_send(3, 1)
    w_x_relay(1, h_a)
    y_done(1, 0)
    y_done(1, 1)
    sparse(1, 0)
    sparse(1, 1)
    s_x4()
    w_b_done()
    w_x(2, h_b)
    w_far_done()
    w_x(3, h_o)
    w_x_done(1, h_a)
    s_swap()
    y_relay(3, 0)
    w_x_relay(2, h_b)
    w_x_relay(3, h_o)
    y_done(2, 0)
    y_done(2, 1)
    sparse(2, 0)
    sparse(2, 1)
    w_x_done(2, h_b)
    y_relay(3, 1)
    w_x_done(3, h_o)
    sparse(3, 0, 0, 3)
    s_done()
    dense_part()
    sparse(3, 1, 0, 3)
    y_done(3, 0)
    sparse(3, 0, 3, 4)
    y_done(3, 1)
    sparse(3, 1, 3, 4)
    combine()
    for group, hh in enumerate((h, h_a, h_b, h_o)):
        w_core(group, hh)
    mlp()
    for copy, cond in pending:
        if cond is None:
            copy().wait_send()
        else:
            pl.when(cond)(lambda copy=copy: copy().wait_send())


def shards(features, stripe_owner, dense_weight, sparse_weight, send_blocks, target_block, first_weight, second_weight):
    smem = pl.BlockSpec(memory_space=pltpu.SMEM)
    vmem = pl.BlockSpec(memory_space=pltpu.VMEM)
    hbm = pl.BlockSpec(memory_space=pl.ANY)
    return pl.pallas_call(
        kernel,
        out_shape=jax.ShapeDtypeStruct((512, 512), F32),
        in_specs=[smem, smem, vmem, vmem, vmem, vmem, hbm, hbm],
        out_specs=vmem,
        scratch_shapes=[
            pltpu.VMEM((4, 2, 512, 256), BF),
            pltpu.VMEM((16, 8, 128), F32),
            pltpu.VMEM((32, 16, 128), BF),
            pltpu.VMEM((4, 2, 2, 3, 128, 256), BF),
            pltpu.VMEM((4, 2, 4, 3, 128, 256), BF),
            pltpu.VMEM((16, 512, 256), BF),
            pltpu.VMEM((4, 4, 2, 16, 2048), BF),
            pltpu.VMEM((4, 4, 2, 64, 512), BF),
            pltpu.VMEM((512, 512), BF),
            pltpu.VMEM((4, 128, 512), BF),
            pltpu.VMEM((2, 64, 512), BF),
            pltpu.VMEM((2, 128, 512), BF),
            pltpu.VMEM((4, 32, 512), BF),
            pltpu.VMEM((2, 16, 512), BF),
            pltpu.VMEM((2, 32, 512), BF),
            pltpu.VMEM((2, 4, 4, 32, 512), BF),
            pltpu.VMEM((512, 1024), jnp.int32),
            pltpu.VMEM((16, 128, 128), jnp.int32),
            pltpu.VMEM((512, 1024), BF),
            pltpu.VMEM((512, 512), F32),
            pltpu.VMEM((512, 128), F32),
            pltpu.VMEM((512, 512), BF),
            pltpu.SemaphoreType.DMA((N_SEND,)),
            pltpu.SemaphoreType.DMA((N_RECV,)),
            pltpu.SemaphoreType.DMA((2,)),
        ],
        compiler_params=pltpu.CompilerParams(
            collective_id=0, has_side_effects=True, vmem_limit_bytes=56 * 2**20
        ),
    )(stripe_owner.T, target_block[0].T, features, send_blocks[0].T, first_weight, second_weight, dense_weight, sparse_weight[0]).astype(BF)


def solution(mesh):
    placed = (
        P(("wide", "narrow"), None),
        P(),
        P(("wide", "narrow"), None),
        P(("wide", "narrow"), None, None, None),
        P(("wide", "narrow"), None, None),
        P(("wide", "narrow"), None, None),
        P("wide", None),
        P("wide", None),
    )
    return jax.shard_map(
        shards, mesh=mesh, in_specs=placed, out_specs=P(("wide", "narrow"), None), check_vma=False
    )
```
